128 devices in a mesh: blk: 8 (over x_lo, y), row: 16 (over x_hi, z, core).
Axes of the slice: x: 4 (x_hi: 2, x_lo: 2; x = x_hi * 2 + x_lo), y: 4, z: 4, core: 2. Of those that a mesh axis runs over, the one named last changes fastest.
Arguments:
- intersection: bfloat16 [4096, 4096], P('row', 'blk'), may hold values from -0.09375 to 0.09375
- inverse_dev: bfloat16 [4096, 4096], P('row', 'blk'), may hold values from -0.09375 to 0.09375
- hamiltonian: bfloat16 [4096, 4096], P('row', 'blk'), may hold values from -0.0625 to 0.0625
- chem_potential: float32 [1], replicated, may hold values from -0.4 to 0.4
- pattern_s: int32 [32, 32], replicated, may hold values 0 or 1
- pattern_z: int32 [32, 32], replicated, may hold values 0 or 1
- pattern_h: int32 [32, 32], replicated, may hold values 0 or 1
- fill_inverse: int32 [32, 32], replicated, may hold values 0 or 1
- fill_sign: int32 [32, 32], replicated, may hold values 0 or 1
Outputs:
- refined_inverse: bfloat16 [4096, 4096], P('row', 'blk')
- inverse_error: bfloat16 [4096, 4096], P('row', 'blk')
- sign_step: bfloat16 [4096, 4096], P('row', 'blk')
The draws below stay inside these ranges and needn't reach their ends.
All inputs are finite; a program needn't handle non-finite values.
Results may differ from the reference program's by a relative error of at most 0.0067.
Values may be sent and summed in bfloat16 or wider, within the bound.
No kernel may reach another device: no remote copies, remote signals or barrier semaphores. Data moves between devices by JAX's collectives and lax.ppermute only.
A program may use at most 64 MiB of HBM per device.

```python
import jax
import jax.numpy as jnp
from jax import lax

BS = 128
NB = 32
N = 4096


def touch_ends(entries, stream_key, smallest, high):
    place = [jax.random.randint(jax.random.fold_in(stream_key, axis), (), 0, length) for axis, length in enumerate(entries.shape)]
    widest = entries.shape.index(max(entries.shape))
    next_to = place[:widest] + [(place[widest] + 1) % entries.shape[widest]] + place[widest + 1:]
    return entries.at[tuple(place)].set(smallest).at[tuple(next_to)].set(high)


def steps_of(rng, shape, shards, low, high):
    factor_of = 1.0
    for dim, parts in shards:
        steps = jax.random.uniform(jax.random.fold_in(jax.random.fold_in(rng, 6), dim), (parts,), jnp.float32, low / len(shards), high / len(shards))
        factor_of = factor_of * jnp.repeat(jnp.exp(steps), shape[dim] // parts).reshape((-1,) + (1,) * (len(shape) - 1 - dim))
    return factor_of


def centred(own_key, shape, deviation, most, cuts=(), kind=jnp.bfloat16):
    loudness = steps_of(own_key, shape, cuts, -0.22, 0.18) if cuts else 1.0
    result = jax.random.normal(own_key, shape, jnp.float32) * deviation * loudness
    return jnp.minimum(jnp.maximum(result, -most), most).astype(kind)


def setup_inputs(seed: int = 0) -> dict:
    arg_keys = jax.random.split(jax.random.key(seed), 10)
    return {
        "intersection": centred(arg_keys[0], (N, N), N ** -0.5, 0.09375, ((0, 16), (1, 8))),
        "inverse_dev": centred(arg_keys[1], (N, N), N ** -0.5, 0.09375, ((0, 16), (1, 8))),
        "hamiltonian": centred(arg_keys[2], (N, N), (2 * N) ** -0.5, 0.0625, ((0, 16), (1, 8))),
        "chem_potential": jnp.clip(jax.random.uniform(arg_keys[3], (1,), jnp.float32, -0.4, 0.4), -0.4, 0.4),
        "pattern_s": touch_ends((jax.random.randint(arg_keys[4], (NB, NB), 0, 2) < 1).astype(jnp.int32), jax.random.fold_in(arg_keys[4], 1), 0, 1),
        "pattern_z": touch_ends((jax.random.randint(arg_keys[5], (NB, NB), 0, 2) < 1).astype(jnp.int32), jax.random.fold_in(arg_keys[5], 1), 0, 1),
        "pattern_h": touch_ends((jax.random.randint(arg_keys[6], (NB, NB), 0, 2) < 1).astype(jnp.int32), jax.random.fold_in(arg_keys[6], 1), 0, 1),
        "fill_inverse": touch_ends((jax.random.randint(arg_keys[7], (NB, NB), 0, 4) < 3).astype(jnp.int32), jax.random.fold_in(arg_keys[7], 1), 0, 1),
        "fill_sign": touch_ends((jax.random.randint(arg_keys[8], (NB, NB), 0, 4) < 3).astype(jnp.int32), jax.random.fold_in(arg_keys[8], 1), 0, 1),
    }


def expand(pattern):
    wide = jnp.repeat(jnp.repeat(pattern.astype(jnp.float32), BS, axis=0), BS, axis=1)
    return wide


def product(left, right):
    return jnp.dot(left.astype(jnp.float32), right.astype(jnp.float32), precision=lax.Precision.HIGHEST)


def reference(intersection, inverse_dev, hamiltonian, chem_potential, pattern_s, pattern_z, pattern_h, fill_inverse, fill_sign):
    ident = jnp.eye(N, dtype=jnp.float32)
    seff = (ident + 0.35 * expand(pattern_s) * intersection.astype(jnp.float32)).astype(jnp.bfloat16)
    zeff = (ident - 0.35 * expand(pattern_z) * inverse_dev.astype(jnp.float32)).astype(jnp.bfloat16)
    heff = (expand(pattern_h) * hamiltonian.astype(jnp.float32)).astype(jnp.bfloat16)
    first = product(zeff, seff).astype(jnp.bfloat16)
    second = product(first, zeff)
    refined = (expand(fill_inverse) * (2.0 * zeff.astype(jnp.float32) - second)).astype(jnp.bfloat16)
    error = (ident - product(refined, seff)).astype(jnp.bfloat16)
    mask_sign = expand(fill_sign)
    shifted = (mask_sign * product(refined, heff) - chem_potential[0] * ident).astype(jnp.bfloat16)
    square = (mask_sign * product(shifted, shifted)).astype(jnp.bfloat16)
    cube = product(shifted, square)
    sign = (0.5 * (3.0 * shifted.astype(jnp.float32) - cube)).astype(jnp.bfloat16)
    return refined, error, sign
```

```python
import functools

import jax
import jax.numpy as jnp
from jax import lax
from jax.experimental import pallas as pl
from jax.experimental.pallas import tpu as pltpu
from jax.sharding import PartitionSpec as P


BS = 128
AXES = ("blk", "row")
BF = jnp.bfloat16
F32 = jnp.float32
VMEM_LIMIT = 10 * 2**20


def flat(x, y, z, c):
    x, y, z = x % 4, y % 4, z % 4
    return ((x % 2) * 4 + y) * 16 + (x // 2) * 8 + z * 2 + c


def moves(step, step1=None):
    steps = (step, step1 or step)
    return [
        (flat(x, y, z, c), flat(*steps[c](x, y, z, c)))
        for x in range(4)
        for y in range(4)
        for z in range(4)
        for c in range(2)
    ]


def far(x, y, z, c):
    return (x ^ 2, y, z, c)


def z_up(x, y, z, c):
    return (x, y, z + 1, c)


def z_down(x, y, z, c):
    return (x, y, z - 1, c)


NEAR = moves(lambda x, y, z, c: (x ^ 1, y, z, c))
Y_UP = moves(lambda x, y, z, c: (x, y + 1, z, c))
Y_DOWN = moves(lambda x, y, z, c: (x, y - 1, z, c))
Y_TWICE = moves(lambda x, y, z, c: (x, y + 2, z, c))
CORE = moves(lambda x, y, z, c: (x, y, z, 1 - c))
FAR_TWICE = moves(far, lambda x, y, z, c: (x, y, z + 2, c))
UP_DOWN = moves(z_up, z_down)
UP_FAR = moves(z_up, far)
DOWN_STAY = moves(z_down, lambda x, y, z, c: (x, y, z, c))


def send(array, pairs):
    return lax.ppermute(array, AXES, pairs)


def gather_rows(own, relay):
    other = send(own, NEAR)
    below = send(own, Y_UP)
    above = send(own, Y_DOWN)
    other_below = send(other, Y_UP)
    other_above = send(other, Y_DOWN)
    if relay:
        below2 = send(below, Y_UP)
        other2 = send(other_above, Y_DOWN)
    else:
        below2 = send(own, Y_TWICE)
        other2 = send(below2, NEAR)
    return [
        (own, (0, 0)),
        (other, (1, 0)),
        (below, (0, -1)),
        (above, (0, 1)),
        (other_below, (1, -1)),
        (other_above, (1, 1)),
        (below2, (0, 2)),
        (other2, (1, 2)),
    ]


def gather_cols(own):
    half = send(own, CORE)
    block = jnp.concatenate([own, half], 0)
    d0 = send(block, FAR_TWICE)
    d1 = send(block, UP_DOWN)
    d2 = send(d0, UP_FAR)
    d3 = send(d0, DOWN_STAY)
    got = [send(d, CORE) for d in (d0, d1, d2, d3)]
    return [
        (own, half, (0, 0), (0, 0)),
        (d0, got[0], (1, 0), (0, 2)),
        (d1, got[1], (0, -1), (0, 1)),
        (d2, got[2], (1, -1), (1, 2)),
        (d3, got[3], (1, 1), None),
    ]


def place():
    row = lax.axis_index("row")
    blk = lax.axis_index("blk")
    return row, blk


def keep(pattern, row, blk, value):
    rows = []
    for i in range(2):
        cells = []
        for j in range(4):
            on = pattern[row * 2 + i, blk * 4 + j].astype(F32)
            cells.append(value[i * BS : (i + 1) * BS, j * BS : (j + 1) * BS] * on)
        rows.append(jnp.concatenate(cells, 1))
    return jnp.concatenate(rows, 0)


def identity(row, blk, shape):
    below = lax.broadcasted_iota(jnp.int32, shape, 0) + row * shape[0]
    along = lax.broadcasted_iota(jnp.int32, shape, 1) + blk * shape[1]
    return (below == along).astype(F32)


VMEM = pl.BlockSpec(memory_space=pltpu.VMEM)
ANY = pl.BlockSpec(memory_space=pl.ANY)


def fetch(given, held, sems):
    copies = [
        pltpu.make_async_copy(one, two, sems.at[k])
        for k, (one, two) in enumerate(zip(given, held))
    ]
    for copy in copies:
        copy.start()
    for copy in copies:
        copy.wait()


def prepare_body(*refs):
    given, outs, held, sems = refs[:4], refs[4:6], refs[6:10], refs[10]
    fetch(given, held, sems)
    ps, pz, s, z = held
    row, blk = place()
    ident = identity(row, blk, s.shape)
    outs[0][...] = (ident + 0.35 * keep(ps, row, blk, s[...].astype(F32))).astype(BF)
    outs[1][...] = (ident - 0.35 * keep(pz, row, blk, z[...].astype(F32))).astype(BF)


def prepare(ps, pz, s, z):
    out = jax.ShapeDtypeStruct(s.shape, BF)
    return pl.pallas_call(
        prepare_body,
        out_shape=(out, out),
        in_specs=[ANY] * 4,
        out_specs=[VMEM] * 2,
        scratch_shapes=[pltpu.SMEM(ps.shape, jnp.int32)] * 2
        + [pltpu.VMEM(s.shape, BF)] * 2
        + [pltpu.SemaphoreType.DMA((4,))],
        name="prepare",
    )(ps, pz, s, z)


def late_body(*refs):
    given, outs, held, sems = refs[:5], refs[5:9], refs[9:14], refs[14]
    fetch(given, held, sems)
    ph, fi, fs, mu, h = held
    row, blk = place()
    ones = jnp.ones(h.shape, F32)
    outs[0][...] = keep(ph, row, blk, h[...].astype(F32)).astype(BF)
    outs[1][...] = keep(fi, row, blk, ones).astype(BF)
    outs[2][...] = keep(fs, row, blk, ones).astype(BF)
    outs[3][...] = jnp.full(outs[3].shape, mu[0], F32)


def prepare_late(ph, fi, fs, mu, h):
    out = jax.ShapeDtypeStruct(h.shape, BF)
    return pl.pallas_call(
        late_body,
        out_shape=(out, out, out, jax.ShapeDtypeStruct((8, BS), F32)),
        in_specs=[ANY] * 5,
        out_specs=[VMEM] * 4,
        scratch_shapes=[pltpu.SMEM(ph.shape, jnp.int32)] * 3
        + [pltpu.SMEM((1,), F32), pltpu.VMEM(h.shape, BF)]
        + [pltpu.SemaphoreType.DMA((5,))],
        name="prepare_late",
    )(ph, fi, fs, mu, h)


def product_body(finish, n_extra, n_out, a_sources, b_sources, *refs):
    extras, refs = refs[:n_extra], refs[n_extra:]
    a_refs, refs = refs[: len(a_sources)], refs[len(a_sources) :]
    b_refs, refs = refs[: 2 * len(b_sources)], refs[2 * len(b_sources) :]
    outs, refs = refs[:n_out], refs[n_out:]
    b_held, sems = refs
    row, blk = place()
    core = row % 2
    xh, z = row // 8, (row // 2) % 4
    xl, y = blk // 4, blk % 4
    rows = a_refs[0].shape[0]

    def start_of(bit, ring, source):
        return (((bit + source[0]) % 2) * 4 + (ring + source[1] + 4) % 4) * (2 * rows)

    waits = []

    def bring(ref, fetcher, source):
        at = start_of(xh, z, source)
        for k in range(ref.shape[0] // rows):
            half = fetcher if k == 0 else 1 - fetcher
            copy = pltpu.make_async_copy(
                ref.at[pl.ds(k * rows, rows)],
                b_held.at[pl.ds(pl.multiple_of(at + half * rows, rows), rows)],
                sems.at[len(waits)],
            )
            copy.start()
            waits.append(copy)

    def bring_either(here, there, source):
        at = start_of(xh, z, source)
        for k in range(2):
            target = b_held.at[pl.ds(pl.multiple_of(at + k * rows, rows), rows)]
            for side, ref in enumerate((here, there)):
                copy = pltpu.make_async_copy(
                    ref.at[pl.ds(k * rows, rows)], target, sems.at[len(waits)]
                )
                pl.when(core == side)(copy.start)
            waits.append(copy)

    for k, (first, second) in enumerate(b_sources):
        here, there = b_refs[2 * k], b_refs[2 * k + 1]
        if second is None:
            bring_either(here, there, first)
        else:
            one = [jnp.where(core == 0, a, b) for a, b in zip(first, second)]
            two = [jnp.where(core == 0, b, a) for a, b in zip(first, second)]
            bring(here, core, one)
            bring(there, 1 - core, two)
    for copy in waits:
        copy.wait()
    total = None
    for ref, source in zip(a_refs, a_sources):
        at = pl.multiple_of(start_of(xl, y, source), 2 * rows)
        part = jnp.dot(ref[...], b_held[pl.ds(at, 2 * rows)], preferred_element_type=F32)
        total = part if total is None else total + part
    finish(row, blk, total, extras, outs)


def product(finish, a, b, extras=(), n_out=1):
    rows, cols = a[0][0].shape
    out = jax.ShapeDtypeStruct((rows, cols), BF)
    a_sources = [source for _, source in a]
    b_sources = [one[2:] for one in b]
    b_arrays = [array for one in b for array in one[:2]]
    got = pl.pallas_call(
        functools.partial(
            product_body, finish, len(extras), n_out, a_sources, b_sources
        ),
        out_shape=[out] * n_out,
        in_specs=[VMEM] * (len(extras) + len(a) + len(b_arrays)),
        out_specs=[VMEM] * n_out,
        scratch_shapes=[
            pltpu.VMEM((16 * rows, cols), BF),
            pltpu.SemaphoreType.DMA((16,)),
        ],
        compiler_params=pltpu.CompilerParams(vmem_limit_bytes=VMEM_LIMIT),
    )(*extras, *[one[0] for one in a], *b_arrays)
    return got if n_out > 1 else got[0]


def end_first(row, blk, total, extras, outs):
    outs[0][...] = total.astype(BF)


def end_refined(row, blk, total, extras, outs):
    mask, own = extras
    value = mask[...].astype(F32) * (2.0 * own[...].astype(F32) - total)
    outs[0][...] = value.astype(BF)


def end_error(row, blk, total, extras, outs):
    outs[0][...] = (identity(row, blk, total.shape) - total).astype(BF)
    outs[1][...] = extras[0][...]


def end_shifted(row, blk, total, extras, outs):
    mask, mu = extras
    shift = mu[0:1, 0:1] * identity(row, blk, total.shape)
    outs[0][...] = (mask[...].astype(F32) * total - shift).astype(BF)


def end_square(row, blk, total, extras, outs):
    outs[0][...] = (extras[0][...].astype(F32) * total).astype(BF)


def end_sign(row, blk, total, extras, outs):
    outs[0][...] = (0.5 * (3.0 * extras[0][...].astype(F32) - total)).astype(BF)


def body(s, z, h, mu, ps, pz, ph, fi, fs):
    seff, zeff = prepare(ps, pz, s, z)
    heff, keep_inverse, keep_sign, mu = prepare_late(ph, fi, fs, mu, h)
    z_rows = gather_rows(zeff, True)
    s_cols = gather_cols(seff)
    first = product(end_first, z_rows, s_cols)
    f_rows = gather_rows(first, False)
    z_cols = gather_cols(zeff)
    refined = product(end_refined, f_rows, z_cols, (keep_inverse, zeff))
    r_rows = gather_rows(refined, False)
    h_cols = gather_cols(heff)
    shifted = product(end_shifted, r_rows, h_cols, (keep_sign, mu))
    x_rows = gather_rows(shifted, True)
    x_cols = gather_cols(shifted)
    error, refined = product(end_error, r_rows, s_cols, (refined,), 2)
    square = product(end_square, x_rows, x_cols, (keep_sign,))
    q_cols = gather_cols(square)
    sign = product(end_sign, x_rows, q_cols, (shifted,))
    return refined, error, sign


def solution(mesh):
    placed = (P("row", "blk"), P("row", "blk"), P("row", "blk"), P(), P(), P(), P(), P(), P())
    return jax.shard_map(
        body,
        mesh=mesh,
        in_specs=placed,
        out_specs=(P("row", "blk"), P("row", "blk"), P("row", "blk")),
        check_vma=False,
    )
```

```python
import functools

import jax
import jax.numpy as jnp
from jax import lax
from jax.experimental import pallas as pl
from jax.experimental.pallas import tpu as pltpu
from jax.sharding import PartitionSpec as P


BS = 128
AXES = ("blk", "row")
BF = jnp.bfloat16
F32 = jnp.float32
VMEM_LIMIT = 10 * 2**20
TIGHT = 64 * 2**20 - 600 * 2**10
TIGHT_LATE = 60 * 2**20


def flat(x, y, z, c):
    x, y, z = x % 4, y % 4, z % 4
    return ((x % 2) * 4 + y) * 16 + (x // 2) * 8 + z * 2 + c


def moves(step, step1=None):
    steps = (step, step1 or step)
    return [
        (flat(x, y, z, c), flat(*steps[c](x, y, z, c)))
        for x in range(4)
        for y in range(4)
        for z in range(4)
        for c in range(2)
    ]


def far(x, y, z, c):
    return (x ^ 2, y, z, c)


def z_up(x, y, z, c):
    return (x, y, z + 1, c)


def z_down(x, y, z, c):
    return (x, y, z - 1, c)


NEAR = moves(lambda x, y, z, c: (x ^ 1, y, z, c))
Y_UP = moves(lambda x, y, z, c: (x, y + 1, z, c))
Y_DOWN = moves(lambda x, y, z, c: (x, y - 1, z, c))
Y_TWICE = moves(lambda x, y, z, c: (x, y + 2, z, c))
CORE = moves(lambda x, y, z, c: (x, y, z, 1 - c))
FAR_TWICE = moves(far, lambda x, y, z, c: (x, y, z + 2, c))
UP_DOWN = moves(z_up, z_down)
UP_FAR = moves(z_up, far)
DOWN_SWAP = moves(lambda x, y, z, c: (x, y, z - 1, 1), lambda x, y, z, c: (x, y, z, 0))


def send(array, pairs):
    return lax.ppermute(array, AXES, pairs)


def gather_rows(own, relay):
    other = send(own, NEAR)
    below = send(own, Y_UP)
    above = send(own, Y_DOWN)
    other_below = send(other, Y_UP)
    other_above = send(other, Y_DOWN)
    if relay:
        below2 = send(below, Y_UP)
        other2 = send(other_above, Y_DOWN)
    else:
        below2 = send(own, Y_TWICE)
        other2 = send(below2, NEAR)
    return [
        (own, (0, 0)),
        (other, (1, 0)),
        (below, (0, -1)),
        (above, (0, 1)),
        (other_below, (1, -1)),
        (other_above, (1, 1)),
        (below2, (0, 2)),
        (other2, (1, 2)),
    ]


def gather_cols(own):
    half = send(own, CORE)
    block = jnp.concatenate([own, half], 0)
    d0 = send(block, FAR_TWICE)
    d1 = send(block, UP_DOWN)
    d2 = send(d0, UP_FAR)
    d3 = send(d0, DOWN_SWAP)
    got = [send(d, CORE) for d in (d0, d1, d2, d3)]
    return [
        (own, half, (0, 0), (0, 0)),
        (d0, got[0], (1, 0), (0, 2)),
        (d1, got[1], (0, -1), (0, 1)),
        (d2, got[2], (1, -1), (1, 2)),
        (got[3], d3, (1, 1), None),
    ]


def place():
    row = lax.axis_index("row")
    blk = lax.axis_index("blk")
    return row, blk


def keep(pattern, row, blk, value):
    rows = []
    for i in range(2):
        cells = []
        for j in range(4):
            on = pattern[row * 2 + i, blk * 4 + j].astype(F32)
            cells.append(value[i * BS : (i + 1) * BS, j * BS : (j + 1) * BS] * on)
        rows.append(jnp.concatenate(cells, 1))
    return jnp.concatenate(rows, 0)


def identity(row, blk, shape):
    below = lax.broadcasted_iota(jnp.int32, shape, 0) + row * shape[0]
    along = lax.broadcasted_iota(jnp.int32, shape, 1) + blk * shape[1]
    return (below == along).astype(F32)


VMEM = pl.BlockSpec(memory_space=pltpu.VMEM)
ANY = pl.BlockSpec(memory_space=pl.ANY)


def fetch(given, held, sems):
    copies = [
        pltpu.make_async_copy(one, two, sems.at[k])
        for k, (one, two) in enumerate(zip(given, held))
    ]
    for copy in copies:
        copy.start()
    for copy in copies:
        copy.wait()


def prepare_body(*refs):
    given, outs, held, sems = refs[:4], refs[4:6], refs[6:10], refs[10]
    fetch(given, held, sems)
    ps, pz, s, z = held
    row, blk = place()
    ident = identity(row, blk, s.shape)
    outs[0][...] = (ident + 0.35 * keep(ps, row, blk, s[...].astype(F32))).astype(BF)
    outs[1][...] = (ident - 0.35 * keep(pz, row, blk, z[...].astype(F32))).astype(BF)


def prepare(ps, pz, s, z):
    out = jax.ShapeDtypeStruct(s.shape, BF)
    return pl.pallas_call(
        prepare_body,
        out_shape=(out, out),
        in_specs=[ANY] * 4,
        out_specs=[VMEM] * 2,
        scratch_shapes=[pltpu.SMEM(ps.shape, jnp.int32)] * 2
        + [pltpu.VMEM(s.shape, BF)] * 2
        + [pltpu.SemaphoreType.DMA((4,))],
        name="prepare",
        compiler_params=pltpu.CompilerParams(vmem_limit_bytes=TIGHT),
    )(ps, pz, s, z)


def late_body(*refs):
    given, outs, held, sems = refs[:5], refs[5:9], refs[9:14], refs[14]
    fetch(given, held, sems)
    ph, fi, fs, mu, h = held
    row, blk = place()
    ones = jnp.ones(h.shape, F32)
    outs[0][...] = keep(ph, row, blk, h[...].astype(F32)).astype(BF)
    outs[1][...] = keep(fi, row, blk, ones).astype(BF)
    outs[2][...] = keep(fs, row, blk, ones).astype(BF)
    outs[3][...] = jnp.full(outs[3].shape, mu[0], F32)


def prepare_late(ph, fi, fs, mu, h):
    out = jax.ShapeDtypeStruct(h.shape, BF)
    return pl.pallas_call(
        late_body,
        out_shape=(out, out, out, jax.ShapeDtypeStruct((8, BS), F32)),
        in_specs=[ANY] * 5,
        out_specs=[VMEM] * 4,
        scratch_shapes=[pltpu.SMEM(ph.shape, jnp.int32)] * 3
        + [pltpu.SMEM((1,), F32), pltpu.VMEM(h.shape, BF)]
        + [pltpu.SemaphoreType.DMA((5,))],
        name="prepare_late",
        compiler_params=pltpu.CompilerParams(vmem_limit_bytes=TIGHT_LATE),
    )(ph, fi, fs, mu, h)


def product_body(finish, n_extra, n_out, a_sources, b_sources, *refs):
    extras, refs = refs[:n_extra], refs[n_extra:]
    a_refs, refs = refs[: len(a_sources)], refs[len(a_sources) :]
    b_refs, refs = refs[: 2 * len(b_sources)], refs[2 * len(b_sources) :]
    outs, refs = refs[:n_out], refs[n_out:]
    b_held, sems = refs
    row, blk = place()
    core = row % 2
    xh, z = row // 8, (row // 2) % 4
    xl, y = blk // 4, blk % 4
    rows = a_refs[0].shape[0]

    def start_of(bit, ring, source):
        return (((bit + source[0]) % 2) * 4 + (ring + source[1] + 4) % 4) * (2 * rows)

    waits = []

    def bring(ref, fetcher, source):
        at = start_of(xh, z, source)
        for k in range(ref.shape[0] // rows):
            half = fetcher if k == 0 else 1 - fetcher
            copy = pltpu.make_async_copy(
                ref.at[pl.ds(k * rows, rows)],
                b_held.at[pl.ds(pl.multiple_of(at + half * rows, rows), rows)],
                sems.at[len(waits)],
            )
            copy.start()
            waits.append(copy)

    def bring_either(here, there, source):
        at = start_of(xh, z, source)
        for k in range(2):
            target = b_held.at[pl.ds(pl.multiple_of(at + k * rows, rows), rows)]
            for side, ref in enumerate((here, there)):
                copy = pltpu.make_async_copy(
                    ref.at[pl.ds(k * rows, rows)], target, sems.at[len(waits)]
                )
                pl.when(core == side)(copy.start)
            waits.append(copy)

    for k, (first, second) in enumerate(b_sources):
        here, there = b_refs[2 * k], b_refs[2 * k + 1]
        if second is None:
            bring_either(here, there, first)
        else:
            one = [jnp.where(core == 0, a, b) for a, b in zip(first, second)]
            two = [jnp.where(core == 0, b, a) for a, b in zip(first, second)]
            bring(here, core, one)
            bring(there, 1 - core, two)
    for copy in waits:
        copy.wait()
    total = None
    for ref, source in zip(a_refs, a_sources):
        at = pl.multiple_of(start_of(xl, y, source), 2 * rows)
        part = jnp.dot(ref[...], b_held[pl.ds(at, 2 * rows)], preferred_element_type=F32)
        total = part if total is None else total + part
    finish(row, blk, total, extras, outs)


def product(finish, a, b, extras=(), n_out=1):
    rows, cols = a[0][0].shape
    out = jax.ShapeDtypeStruct((rows, cols), BF)
    a_sources = [source for _, source in a]
    b_sources = [one[2:] for one in b]
    b_arrays = [array for one in b for array in one[:2]]
    got = pl.pallas_call(
        functools.partial(
            product_body, finish, len(extras), n_out, a_sources, b_sources
        ),
        out_shape=[out] * n_out,
        in_specs=[VMEM] * (len(extras) + len(a) + len(b_arrays)),
        out_specs=[VMEM] * n_out,
        scratch_shapes=[
            pltpu.VMEM((16 * rows, cols), BF),
            pltpu.SemaphoreType.DMA((16,)),
        ],
        compiler_params=pltpu.CompilerParams(vmem_limit_bytes=VMEM_LIMIT),
    )(*extras, *[one[0] for one in a], *b_arrays)
    return got if n_out > 1 else got[0]


def end_first(row, blk, total, extras, outs):
    outs[0][...] = total.astype(BF)


def end_refined(row, blk, total, extras, outs):
    mask, own = extras
    value = mask[...].astype(F32) * (2.0 * own[...].astype(F32) - total)
    outs[0][...] = value.astype(BF)


def end_error(row, blk, total, extras, outs):
    outs[0][...] = (identity(row, blk, total.shape) - total).astype(BF)
    outs[1][...] = extras[0][...]


def end_shifted(row, blk, total, extras, outs):
    mask, mu = extras
    shift = mu[0:1, 0:1] * identity(row, blk, total.shape)
    outs[0][...] = (mask[...].astype(F32) * total - shift).astype(BF)


def end_square(row, blk, total, extras, outs):
    outs[0][...] = (extras[0][...].astype(F32) * total).astype(BF)


def end_sign(row, blk, total, extras, outs):
    outs[0][...] = (0.5 * (3.0 * extras[0][...].astype(F32) - total)).astype(BF)


def body(s, z, h, mu, ps, pz, ph, fi, fs):
    seff, zeff = prepare(ps, pz, s, z)
    heff, keep_inverse, keep_sign, mu = prepare_late(ph, fi, fs, mu, h)
    z_rows = gather_rows(zeff, False)
    s_cols = gather_cols(seff)
    first = product(end_first, z_rows, s_cols)
    f_rows = gather_rows(first, False)
    z_cols = gather_cols(zeff)
    refined = product(end_refined, f_rows, z_cols, (keep_inverse, zeff))
    r_rows = gather_rows(refined, False)
    h_cols = gather_cols(heff)
    shifted = product(end_shifted, r_rows, h_cols, (keep_sign, mu))
    x_rows = gather_rows(shifted, False)
    x_cols = gather_cols(shifted)
    error, refined = product(end_error, r_rows, s_cols, (refined,), 2)
    square = product(end_square, x_rows, x_cols, (keep_sign,))
    q_cols = gather_cols(square)
    sign = product(end_sign, x_rows, q_cols, (shifted,))
    return refined, error, sign


def solution(mesh):
    placed = (P("row", "blk"), P("row", "blk"), P("row", "blk"), P(), P(), P(), P(), P(), P())
    return jax.shard_map(
        body,
        mesh=mesh,
        in_specs=placed,
        out_specs=(P("row", "blk"), P("row", "blk"), P("row", "blk")),
        check_vma=False,
    )
```

```python
import functools

import jax
import jax.numpy as jnp
from jax import lax
from jax.experimental import pallas as pl
from jax.experimental.pallas import tpu as pltpu
from jax.sharding import PartitionSpec as P


BS = 128
AXES = ("blk", "row")
BF = jnp.bfloat16
F32 = jnp.float32
VMEM_LIMIT = 10 * 2**20
TIGHT = 60 * 2**20


def flat(x, y, z, c):
    x, y, z = x % 4, y % 4, z % 4
    return ((x % 2) * 4 + y) * 16 + (x // 2) * 8 + z * 2 + c


def moves(step, step1=None):
    steps = (step, step1 or step)
    return [
        (flat(x, y, z, c), flat(*steps[c](x, y, z, c)))
        for x in range(4)
        for y in range(4)
        for z in range(4)
        for c in range(2)
    ]


def far(x, y, z, c):
    return (x ^ 2, y, z, c)


def z_up(x, y, z, c):
    return (x, y, z + 1, c)


def z_down(x, y, z, c):
    return (x, y, z - 1, c)


NEAR = moves(lambda x, y, z, c: (x ^ 1, y, z, c))
Y_UP = moves(lambda x, y, z, c: (x, y + 1, z, c))
Y_DOWN = moves(lambda x, y, z, c: (x, y - 1, z, c))
Y_TWICE = moves(lambda x, y, z, c: (x, y + 2, z, c))
CORE = moves(lambda x, y, z, c: (x, y, z, 1 - c))
FAR_TWICE = moves(far, lambda x, y, z, c: (x, y, z + 2, c))
UP_DOWN = moves(z_up, z_down)
UP_FAR = moves(z_up, far)
DOWN_SWAP = moves(lambda x, y, z, c: (x, y, z - 1, 1), lambda x, y, z, c: (x, y, z, 0))


def send(array, pairs):
    return lax.ppermute(array, AXES, pairs)


def gather_rows(own, relay):
    other = send(own, NEAR)
    below = send(own, Y_UP)
    above = send(own, Y_DOWN)
    other_below = send(other, Y_UP)
    other_above = send(other, Y_DOWN)
    if relay:
        below2 = send(below, Y_UP)
        other2 = send(other_above, Y_DOWN)
    else:
        below2 = send(own, Y_TWICE)
        other2 = send(below2, NEAR)
    return [
        (own, (0, 0)),
        (other, (1, 0)),
        (below, (0, -1)),
        (above, (0, 1)),
        (other_below, (1, -1)),
        (other_above, (1, 1)),
        (below2, (0, 2)),
        (other2, (1, 2)),
    ]


def gather_cols(own):
    half = send(own, CORE)
    block = jnp.concatenate([own, half], 0)
    d0 = send(block, FAR_TWICE)
    d1 = send(block, UP_DOWN)
    d2 = send(d0, UP_FAR)
    d3 = send(d0, DOWN_SWAP)
    got = [send(d, CORE) for d in (d0, d1, d2, d3)]
    return [
        (own, half, (0, 0), (0, 0)),
        (d0, got[0], (1, 0), (0, 2)),
        (d1, got[1], (0, -1), (0, 1)),
        (d2, got[2], (1, -1), (1, 2)),
        (got[3], d3, (1, 1), None),
    ]


def place():
    row = lax.axis_index("row")
    blk = lax.axis_index("blk")
    return row, blk


def keep(pattern, row, blk, value):
    rows = []
    for i in range(2):
        cells = []
        for j in range(4):
            on = pattern[row * 2 + i, blk * 4 + j].astype(F32)
            cells.append(value[i * BS : (i + 1) * BS, j * BS : (j + 1) * BS] * on)
        rows.append(jnp.concatenate(cells, 1))
    return jnp.concatenate(rows, 0)


def identity(row, blk, shape):
    below = lax.broadcasted_iota(jnp.int32, shape, 0) + row * shape[0]
    along = lax.broadcasted_iota(jnp.int32, shape, 1) + blk * shape[1]
    return (below == along).astype(F32)


VMEM = pl.BlockSpec(memory_space=pltpu.VMEM)
ANY = pl.BlockSpec(memory_space=pl.ANY)


def fetch(given, held, sems):
    copies = [
        pltpu.make_async_copy(one, two, sems.at[k])
        for k, (one, two) in enumerate(zip(given, held))
    ]
    for copy in copies:
        copy.start()
    for copy in copies:
        copy.wait()


def prepare_body(*refs):
    given, outs, held, sems = refs[:4], refs[4:6], refs[6:10], refs[10]
    fetch(given, held, sems)
    ps, pz, s, z = held
    row, blk = place()
    ident = identity(row, blk, s.shape)
    outs[0][...] = (ident + 0.35 * keep(ps, row, blk, s[...].astype(F32))).astype(BF)
    outs[1][...] = (ident - 0.35 * keep(pz, row, blk, z[...].astype(F32))).astype(BF)


def prepare(ps, pz, s, z):
    out = pltpu.VMEM(s.shape, BF)
    return pl.pallas_call(
        prepare_body,
        out_shape=(out, out),
        in_specs=[ANY] * 4,
        out_specs=[VMEM] * 2,
        scratch_shapes=[pltpu.SMEM(ps.shape, jnp.int32)] * 2
        + [pltpu.VMEM(s.shape, BF)] * 2
        + [pltpu.SemaphoreType.DMA((4,))],
        name="prepare",
        compiler_params=pltpu.CompilerParams(vmem_limit_bytes=TIGHT),
    )(ps, pz, s, z)


def late_body(*refs):
    given, outs, held, sems = refs[:5], refs[5:9], refs[9:14], refs[14]
    fetch(given, held, sems)
    ph, fi, fs, mu, h = held
    row, blk = place()
    ones = jnp.ones(h.shape, F32)
    outs[0][...] = keep(ph, row, blk, h[...].astype(F32)).astype(BF)
    outs[1][...] = keep(fi, row, blk, ones).astype(BF)
    outs[2][...] = keep(fs, row, blk, ones).astype(BF)
    outs[3][...] = jnp.full(outs[3].shape, mu[0], F32)


def prepare_late(ph, fi, fs, mu, h):
    out = pltpu.VMEM(h.shape, BF)
    return pl.pallas_call(
        late_body,
        out_shape=(out, out, out, pltpu.VMEM((8, BS), F32)),
        in_specs=[ANY] * 5,
        out_specs=[VMEM] * 4,
        scratch_shapes=[pltpu.SMEM(ph.shape, jnp.int32)] * 3
        + [pltpu.SMEM((1,), F32), pltpu.VMEM(h.shape, BF)]
        + [pltpu.SemaphoreType.DMA((5,))],
        name="prepare_late",
        compiler_params=pltpu.CompilerParams(vmem_limit_bytes=TIGHT),
    )(ph, fi, fs, mu, h)


def product_body(finish, n_extra, n_out, a_sources, b_sources, *refs):
    extras, refs = refs[:n_extra], refs[n_extra:]
    a_refs, refs = refs[: len(a_sources)], refs[len(a_sources) :]
    b_refs, refs = refs[: 2 * len(b_sources)], refs[2 * len(b_sources) :]
    outs, refs = refs[:n_out], refs[n_out:]
    b_held, sems = refs
    row, blk = place()
    core = row % 2
    xh, z = row // 8, (row // 2) % 4
    xl, y = blk // 4, blk % 4
    rows = a_refs[0].shape[0]

    def start_of(bit, ring, source):
        return (((bit + source[0]) % 2) * 4 + (ring + source[1] + 4) % 4) * (2 * rows)

    waits = []

    def bring(ref, fetcher, source):
        at = start_of(xh, z, source)
        for k in range(ref.shape[0] // rows):
            half = fetcher if k == 0 else 1 - fetcher
            copy = pltpu.make_async_copy(
                ref.at[pl.ds(k * rows, rows)],
                b_held.at[pl.ds(pl.multiple_of(at + half * rows, rows), rows)],
                sems.at[len(waits)],
            )
            copy.start()
            waits.append(copy)

    def bring_either(here, there, source):
        at = start_of(xh, z, source)
        for k in range(2):
            target = b_held.at[pl.ds(pl.multiple_of(at + k * rows, rows), rows)]
            for side, ref in enumerate((here, there)):
                copy = pltpu.make_async_copy(
                    ref.at[pl.ds(k * rows, rows)], target, sems.at[len(waits)]
                )
                pl.when(core == side)(copy.start)
            waits.append(copy)

    for k, (first, second) in enumerate(b_sources):
        here, there = b_refs[2 * k], b_refs[2 * k + 1]
        if second is None:
            bring_either(here, there, first)
        else:
            one = [jnp.where(core == 0, a, b) for a, b in zip(first, second)]
            two = [jnp.where(core == 0, b, a) for a, b in zip(first, second)]
            bring(here, core, one)
            bring(there, 1 - core, two)
    for copy in waits:
        copy.wait()
    total = None
    for ref, source in zip(a_refs, a_sources):
        at = pl.multiple_of(start_of(xl, y, source), 2 * rows)
        part = jnp.dot(ref[...], b_held[pl.ds(at, 2 * rows)], preferred_element_type=F32)
        total = part if total is None else total + part
    finish(row, blk, total, extras, outs)


def product(finish, a, b, extras=(), n_out=1):
    rows, cols = a[0][0].shape
    out = jax.ShapeDtypeStruct((rows, cols), BF)
    a_sources = [source for _, source in a]
    b_sources = [one[2:] for one in b]
    b_arrays = [array for one in b for array in one[:2]]
    got = pl.pallas_call(
        functools.partial(
            product_body, finish, len(extras), n_out, a_sources, b_sources
        ),
        out_shape=[out] * n_out,
        in_specs=[VMEM] * (len(extras) + len(a) + len(b_arrays)),
        out_specs=[VMEM] * n_out,
        scratch_shapes=[
            pltpu.VMEM((16 * rows, cols), BF),
            pltpu.SemaphoreType.DMA((16,)),
        ],
        compiler_params=pltpu.CompilerParams(vmem_limit_bytes=VMEM_LIMIT),
    )(*extras, *[one[0] for one in a], *b_arrays)
    return got if n_out > 1 else got[0]


def end_first(row, blk, total, extras, outs):
    outs[0][...] = total.astype(BF)


def end_refined(row, blk, total, extras, outs):
    mask, own = extras
    value = mask[...].astype(F32) * (2.0 * own[...].astype(F32) - total)
    outs[0][...] = value.astype(BF)


def end_error(row, blk, total, extras, outs):
    outs[0][...] = (identity(row, blk, total.shape) - total).astype(BF)
    outs[1][...] = extras[0][...]


def end_shifted(row, blk, total, extras, outs):
    mask, mu = extras
    shift = mu[0:1, 0:1] * identity(row, blk, total.shape)
    outs[0][...] = (mask[...].astype(F32) * total - shift).astype(BF)


def end_square(row, blk, total, extras, outs):
    outs[0][...] = (extras[0][...].astype(F32) * total).astype(BF)


def end_sign(row, blk, total, extras, outs):
    outs[0][...] = (0.5 * (3.0 * extras[0][...].astype(F32) - total)).astype(BF)


def body(s, z, h, mu, ps, pz, ph, fi, fs):
    seff, zeff = prepare(ps, pz, s, z)
    heff, keep_inverse, keep_sign, mu = prepare_late(ph, fi, fs, mu, h)
    z_rows = gather_rows(zeff, False)
    s_cols = gather_cols(seff)
    first = product(end_first, z_rows, s_cols)
    f_rows = gather_rows(first, False)
    z_cols = gather_cols(zeff)
    refined = product(end_refined, f_rows, z_cols, (keep_inverse, zeff))
    r_rows = gather_rows(refined, False)
    h_cols = gather_cols(heff)
    shifted = product(end_shifted, r_rows, h_cols, (keep_sign, mu))
    x_rows = gather_rows(shifted, False)
    x_cols = gather_cols(shifted)
    error, refined = product(end_error, r_rows, s_cols, (refined,), 2)
    square = product(end_square, x_rows, x_cols, (keep_sign,))
    q_cols = gather_cols(square)
    sign = product(end_sign, x_rows, q_cols, (shifted,))
    return refined, error, sign


def solution(mesh):
    placed = (P("row", "blk"), P("row", "blk"), P("row", "blk"), P(), P(), P(), P(), P(), P())
    return jax.shard_map(
        body,
        mesh=mesh,
        in_specs=placed,
        out_specs=(P("row", "blk"), P("row", "blk"), P("row", "blk")),
        check_vma=False,
    )
```

```python
import functools

import jax
import jax.numpy as jnp
from jax import lax
from jax.experimental import pallas as pl
from jax.experimental.pallas import tpu as pltpu
from jax.sharding import PartitionSpec as P


BS = 128
AXES = ("blk", "row")
BF = jnp.bfloat16
F32 = jnp.float32
VMEM_LIMIT = 10 * 2**20
TIGHT = 60 * 2**20


def flat(x, y, z, c):
    x, y, z = x % 4, y % 4, z % 4
    return ((x % 2) * 4 + y) * 16 + (x // 2) * 8 + z * 2 + c


def moves(step, step1=None):
    steps = (step, step1 or step)
    return [
        (flat(x, y, z, c), flat(*steps[c](x, y, z, c)))
        for x in range(4)
        for y in range(4)
        for z in range(4)
        for c in range(2)
    ]


def far(x, y, z, c):
    return (x ^ 2, y, z, c)


def z_up(x, y, z, c):
    return (x, y, z + 1, c)


def z_down(x, y, z, c):
    return (x, y, z - 1, c)


NEAR = moves(lambda x, y, z, c: (x ^ 1, y, z, c))
Y_UP = moves(lambda x, y, z, c: (x, y + 1, z, c))
Y_DOWN = moves(lambda x, y, z, c: (x, y - 1, z, c))
Y_TWICE = moves(lambda x, y, z, c: (x, y + 2, z, c))
CORE = moves(lambda x, y, z, c: (x, y, z, 1 - c))
FAR_TWICE = moves(far, lambda x, y, z, c: (x, y, z + 2, c))
UP_DOWN = moves(z_up, z_down)
UP_FAR = moves(z_up, far)
DOWN_SWAP = moves(lambda x, y, z, c: (x, y, z - 1, 1), lambda x, y, z, c: (x, y, z, 0))


def send(array, pairs):
    return lax.ppermute(array, AXES, pairs)


def gather_rows(own, relay):
    other = send(own, NEAR)
    below = send(own, Y_UP)
    above = send(own, Y_DOWN)
    other_below = send(other, Y_UP)
    other_above = send(other, Y_DOWN)
    if relay:
        below2 = send(below, Y_UP)
        other2 = send(other_above, Y_DOWN)
    else:
        below2 = send(own, Y_TWICE)
        other2 = send(below2, NEAR)
    return [
        (own, (0, 0)),
        (other, (1, 0)),
        (below, (0, -1)),
        (above, (0, 1)),
        (other_below, (1, -1)),
        (other_above, (1, 1)),
        (below2, (0, 2)),
        (other2, (1, 2)),
    ]


def gather_cols(own):
    half = send(own, CORE)
    block = jnp.concatenate([own, half], 0)
    d0 = send(block, FAR_TWICE)
    d1 = send(block, UP_DOWN)
    d2 = send(d0, UP_FAR)
    d3 = send(d0, DOWN_SWAP)
    got = [send(d, CORE) for d in (d0, d1, d2, d3)]
    return [
        (own, half, (0, 0), (0, 0)),
        (d0, got[0], (1, 0), (0, 2)),
        (d1, got[1], (0, -1), (0, 1)),
        (d2, got[2], (1, -1), (1, 2)),
        (got[3], d3, (1, 1), None),
    ]


def place():
    row = lax.axis_index("row")
    blk = lax.axis_index("blk")
    return row, blk


def keep(pattern, row, blk, value):
    rows = []
    for i in range(2):
        cells = []
        for j in range(4):
            on = pattern[row * 2 + i, blk * 4 + j].astype(F32)
            cells.append(value[i * BS : (i + 1) * BS, j * BS : (j + 1) * BS] * on)
        rows.append(jnp.concatenate(cells, 1))
    return jnp.concatenate(rows, 0)


def identity(row, blk, shape):
    below = lax.broadcasted_iota(jnp.int32, shape, 0) + row * shape[0]
    along = lax.broadcasted_iota(jnp.int32, shape, 1) + blk * shape[1]
    return (below == along).astype(F32)


VMEM = pl.BlockSpec(memory_space=pltpu.VMEM)
ANY = pl.BlockSpec(memory_space=pl.ANY)


def fetch(given, held, sems):
    copies = [
        pltpu.make_async_copy(one, two, sems.at[k])
        for k, (one, two) in enumerate(zip(given, held))
    ]
    for copy in copies:
        copy.start()
    for copy in copies:
        copy.wait()


def prepare_body(*refs):
    given, outs, held, sems = refs[:4], refs[4:6], refs[6:10], refs[10]
    fetch(given, held, sems)
    ps, pz, s, z = held
    row, blk = place()
    ident = identity(row, blk, s.shape)
    outs[0][...] = (ident + 0.35 * keep(ps, row, blk, s[...].astype(F32))).astype(BF)
    outs[1][...] = (ident - 0.35 * keep(pz, row, blk, z[...].astype(F32))).astype(BF)


def prepare(ps, pz, s, z):
    out = pltpu.VMEM(s.shape, BF)
    return pl.pallas_call(
        prepare_body,
        out_shape=(out, out),
        in_specs=[ANY] * 4,
        out_specs=[VMEM] * 2,
        scratch_shapes=[pltpu.SMEM(ps.shape, jnp.int32)] * 2
        + [pltpu.VMEM(s.shape, BF)] * 2
        + [pltpu.SemaphoreType.DMA((4,))],
        name="prepare",
        compiler_params=pltpu.CompilerParams(vmem_limit_bytes=TIGHT),
    )(ps, pz, s, z)


def late_body(*refs):
    given, outs, held, sems = refs[:5], refs[5:9], refs[9:14], refs[14]
    fetch(given, held, sems)
    ph, fi, fs, mu, h = held
    row, blk = place()
    ones = jnp.ones(h.shape, F32)
    outs[0][...] = keep(ph, row, blk, h[...].astype(F32)).astype(BF)
    outs[1][...] = keep(fi, row, blk, ones).astype(BF)
    outs[2][...] = keep(fs, row, blk, ones).astype(BF)
    outs[3][...] = jnp.full(outs[3].shape, mu[0], F32)


def prepare_late(ph, fi, fs, mu, h):
    out = pltpu.VMEM(h.shape, BF)
    return pl.pallas_call(
        late_body,
        out_shape=(out, out, out, pltpu.VMEM((8, BS), F32)),
        in_specs=[ANY] * 5,
        out_specs=[VMEM] * 4,
        scratch_shapes=[pltpu.SMEM(ph.shape, jnp.int32)] * 3
        + [pltpu.SMEM((1,), F32), pltpu.VMEM(h.shape, BF)]
        + [pltpu.SemaphoreType.DMA((5,))],
        name="prepare_late",
        compiler_params=pltpu.CompilerParams(vmem_limit_bytes=TIGHT),
    )(ph, fi, fs, mu, h)


def product_body(finish, n_extra, n_out, a_sources, b_sources, carry, *refs):
    extras, refs = refs[:n_extra], refs[n_extra:]
    a_refs, refs = refs[: len(a_sources)], refs[len(a_sources) :]
    b_refs, refs = refs[: 2 * len(b_sources)], refs[2 * len(b_sources) :]
    outs, refs = refs[:n_out], refs[n_out:]
    a_held, spare, sems = refs
    row, blk = place()
    core = row % 2
    xh, z = row // 8, (row // 2) % 4
    xl, y = blk // 4, blk % 4
    rows = a_refs[0].shape[0]

    def chunk(bit, ring, source):
        return ((bit + source[0]) % 2) * 4 + (ring + source[1] + 4) % 4

    waits = []
    for ref, source in zip(a_refs, a_sources):
        at = 2 * chunk(xl, y, source)
        for k in range(2):
            copy = pltpu.make_async_copy(
                ref.at[:, pl.ds(k * rows, rows)], a_held.at[at + k], sems.at[len(waits)]
            )
            copy.start()
            waits.append(copy)

    split = b_sources[-1][1] is None
    if split:
        for side in range(2):
            copy = pltpu.make_async_copy(b_refs[side - 2], spare, sems.at[len(waits)])
            pl.when(core == side)(copy.start)
        waits.append(copy)
    for copy in waits:
        copy.wait()

    def part(right, first_half, source):
        at = 2 * chunk(xh, z, source)
        left = jnp.concatenate([a_held[at + first_half], a_held[at + 1 - first_half]], 1)
        return jnp.dot(left, right, preferred_element_type=F32)

    parts = [extras[-1][...]] if carry else []
    for k, (first, second) in enumerate(b_sources):
        here, there = b_refs[2 * k], b_refs[2 * k + 1]
        if second is None:
            parts.append(part(spare[...], 0, first))
        elif here.shape[0] == rows:
            parts.append(part(jnp.concatenate([here[...], there[...]], 0), core, first))
        else:
            one = [jnp.where(core == 0, a, b) for a, b in zip(first, second)]
            two = [jnp.where(core == 0, b, a) for a, b in zip(first, second)]
            parts.append(part(here[...], core, one))
            parts.append(part(there[...], 1 - core, two))
    total = functools.reduce(lambda a, b: a + b, parts)
    finish(row, blk, total, extras, outs)


def product(finish, a, b, extras=(), n_out=1, kind=BF, carry=False):
    rows, cols = a[0][0].shape
    out = jax.ShapeDtypeStruct((rows, cols), kind)
    a_sources = [source for _, source in a]
    b_sources = [one[2:] for one in b]
    b_arrays = [array for one in b for array in one[:2]]
    got = pl.pallas_call(
        functools.partial(
            product_body, finish, len(extras), n_out, a_sources, b_sources, carry
        ),
        out_shape=[out] * n_out,
        in_specs=[VMEM] * (len(extras) + len(a) + len(b_arrays)),
        out_specs=[VMEM] * n_out,
        scratch_shapes=[
            pltpu.VMEM((16, rows, cols // 2), BF),
            pltpu.VMEM((2 * rows, cols), BF),
            pltpu.SemaphoreType.DMA((17,)),
        ],
        compiler_params=pltpu.CompilerParams(vmem_limit_bytes=VMEM_LIMIT),
    )(*extras, *[one[0] for one in a], *b_arrays)
    return got if n_out > 1 else got[0]


def end_first(row, blk, total, extras, outs):
    outs[0][...] = total.astype(BF)


def end_early(row, blk, total, extras, outs):
    outs[0][...] = total


def end_refined(row, blk, total, extras, outs):
    mask, own = extras
    value = mask[...].astype(F32) * (2.0 * own[...].astype(F32) - total)
    outs[0][...] = value.astype(BF)


def end_error(row, blk, total, extras, outs):
    outs[0][...] = (identity(row, blk, total.shape) - total).astype(BF)
    outs[1][...] = extras[0][...]


def end_shifted(row, blk, total, extras, outs):
    mask, mu = extras
    shift = mu[0:1, 0:1] * identity(row, blk, total.shape)
    outs[0][...] = (mask[...].astype(F32) * total - shift).astype(BF)


def end_square(row, blk, total, extras, outs):
    outs[0][...] = (extras[0][...].astype(F32) * total).astype(BF)


def end_sign(row, blk, total, extras, outs):
    outs[0][...] = (0.5 * (3.0 * extras[0][...].astype(F32) - total)).astype(BF)


def body(s, z, h, mu, ps, pz, ph, fi, fs):
    seff, zeff = prepare(ps, pz, s, z)
    heff, keep_inverse, keep_sign, mu = prepare_late(ph, fi, fs, mu, h)
    z_rows = gather_rows(zeff, False)
    s_cols = gather_cols(seff)
    first = product(end_first, z_rows, s_cols)
    f_rows = gather_rows(first, False)
    z_cols = gather_cols(zeff)
    refined = product(end_refined, f_rows, z_cols, (keep_inverse, zeff))
    r_rows = gather_rows(refined, False)
    h_cols = gather_cols(heff)
    shifted = product(end_shifted, r_rows, h_cols, (keep_sign, mu))
    x_rows = gather_rows(shifted, False)
    x_cols = gather_cols(shifted)
    error, refined = product(end_error, r_rows, s_cols, (refined,), 2)
    square = product(end_square, x_rows, x_cols, (keep_sign,))
    q_cols = gather_cols(square)
    partial = product(end_early, x_rows, q_cols[:3], kind=F32)
    sign = product(end_sign, x_rows, q_cols[3:], (shifted, partial), carry=True)
    return refined, error, sign


def solution(mesh):
    placed = (P("row", "blk"), P("row", "blk"), P("row", "blk"), P(), P(), P(), P(), P(), P())
    return jax.shard_map(
        body,
        mesh=mesh,
        in_specs=placed,
        out_specs=(P("row", "blk"), P("row", "blk"), P("row", "blk")),
        check_vma=False,
    )
```
